128 devices in a mesh: shards: 16 (over x, y), tensor: 4 (over z), section: 2 (over core).
Axes of the slice: x: 4, y: 4, z: 4, core: 2. Of those that a mesh axis runs over, the one named last changes fastest.
Arguments:
- gradient: bfloat16 [4, 768, 2048], P('section', 'tensor', 'shards'), may hold values from -36 to 36, as said below
- weight: bfloat16 [4, 768, 2048], P('section', 'tensor', 'shards'), may hold values from -0.21875 to 0.21875
- projector: float32 [4, 768, 256], P('section', 'tensor'), may hold values from -0.21875 to 0.21875
- first_moment: float32 [4, 256, 2048], P('section', 'tensor', 'shards'), may hold values from -0.3125 to 0.3125
- squared_moment: float32 [4, 256, 2048], P('section', 'tensor', 'shards'), may hold values from 1e-07 to 1e-05
- step_count: int32 [4], P('section'), may hold values from 1 to 11
- norm_gains: float32 [4, 768], P('section', 'tensor'), may hold values from 0.5 to 1.5
- gain_gradient: float32 [4, 768], P('section', 'tensor'), may hold values from -0.15625 to 0.15625
- gain_first: float32 [4, 768], P('section', 'tensor'), may hold values from -0.046875 to 0.046875
- gain_second: float32 [4, 768], P('section', 'tensor'), may hold values from 1e-08 to 1e-06
Outputs:
- weight_next: bfloat16 [4, 768, 2048], P('section', 'tensor', 'shards')
- fresh_projector: float32 [4, 768, 256], P('section', 'tensor')
- new_first: float32 [4, 256, 2048], P('section', 'tensor', 'shards')
- new_second: float32 [4, 256, 2048], P('section', 'tensor', 'shards')
- new_gains: float32 [4, 768], P('section', 'tensor')
- new_gain_first: float32 [4, 768], P('section', 'tensor')
- new_gain_second: float32 [4, 768], P('section', 'tensor')
The draws below stay inside these ranges and needn't reach their ends.
Inputs may be any that keep to these rules, and one draw needn't show every extreme that they name: `gradient`: gradient entries are finite real numbers.
All inputs are finite; a program needn't handle non-finite values.
Results may differ from the reference program's by a relative error of at most 0.001.
Values sent between devices are 32-bit elements; how exact they have to be, the bound alone decides.
No kernel may reach another device: no remote copies, remote signals or barrier semaphores. Data moves between devices by JAX's collectives and lax.ppermute only.
A program may use at most 64 MiB of HBM per device.

```python
import math
import jax
import jax.numpy as jnp
from jax import lax

D = 768
FF = 2048
R = 256
NS_STEPS = 5
MATS_ALL = 4


def draw_gradient(key, part):
    keys = jax.random.split(key, 3)
    rising_rows = 3.0 ** (jnp.arange(D, dtype=jnp.float32) / D)
    rising_cols = 3.0 ** (jnp.arange(FF, dtype=jnp.float32) / FF)
    row_scale = jnp.exp(jax.random.uniform(keys[0], (MATS_ALL, D, 1), jnp.float32, 0.0, math.log(10.0))) * rising_rows[None, :, None]
    col_scale = jnp.exp(jax.random.uniform(keys[1], (MATS_ALL, 1, FF), jnp.float32, 0.0, math.log(4.0))) * rising_cols[None, None, :]
    base = jnp.clip(jax.random.normal(keys[2], (MATS_ALL, D, FF), jnp.float32), -6.0, 6.0)
    values = 0.01 * base * row_scale * col_scale
    return values.astype(jnp.bfloat16)


def with_ends(drawn, key, least, top_value):
    longest = drawn.shape.index(max(drawn.shape))
    spots = []
    for shift in (0, 1):
        where = [jax.random.randint(jax.random.fold_in(key, axis), (), 0, length) for axis, length in enumerate(drawn.shape)]
        where[longest] = (where[longest] + shift) % drawn.shape[longest]
        spots.append(tuple(where))
    return drawn.at[spots[0]].set(least).at[spots[1]].set(top_value)


def block_scale(stream_key, shape, cuts, least, top_value):
    level = 1.0
    for axis_at, blocks in cuts:
        steps = jax.random.uniform(jax.random.fold_in(jax.random.fold_in(stream_key, 6), axis_at), (blocks,), jnp.float32, least / len(cuts), top_value / len(cuts))
        level = level * jnp.repeat(jnp.exp(steps), shape[axis_at] // blocks).reshape((-1,) + (1,) * (len(shape) - 1 - axis_at))
    return level


def gaussian(own_key, extent, scale, most, cuts=(), held_as=jnp.bfloat16):
    level = block_scale(own_key, extent, cuts, -0.22, 0.18) if cuts else 1.0
    entries = jax.random.normal(own_key, extent, jnp.float32) * scale * level
    return jnp.minimum(jnp.maximum(entries, -most), most).astype(held_as)


def setup_inputs(seed: int = 0) -> dict:
    streams_of = jax.random.split(jax.random.key(seed), 11)
    return {
        "gradient": draw_gradient(jax.random.fold_in(streams_of[10], 71), 0),
        "weight": gaussian(streams_of[1], (MATS_ALL, D, FF), D ** -0.5, 0.21875, ((0, 2), (1, 4), (2, 16))),
        "projector": gaussian(streams_of[2], (MATS_ALL, D, R), D ** -0.5, 0.21875, ((0, 2), (1, 4)), jnp.float32),
        "first_moment": gaussian(streams_of[3], (MATS_ALL, R, FF), 0.02, 0.3125, ((0, 2), (1, 4), (2, 16)), jnp.float32),
        "squared_moment": jnp.clip(jnp.exp(math.log(9.999999747378752e-06) - 4.6051701 * jax.random.uniform(streams_of[4], (MATS_ALL, R, FF), jnp.float32) ** block_scale(streams_of[4], (MATS_ALL, R, FF), ((0, 2), (1, 4), (2, 16)), -0.2, 0.2)), 1.0000000116860974e-07, 9.999999747378752e-06),
        "step_count": with_ends(jax.random.randint(streams_of[5], (MATS_ALL,), 1, 12), jax.random.fold_in(streams_of[5], 1), 1, 11).astype(jnp.int32),
        "norm_gains": jnp.clip(1.0 + 0.1 * jax.random.normal(streams_of[6], (MATS_ALL, D), jnp.float32), 0.5, 1.5),
        "gain_gradient": gaussian(streams_of[7], (MATS_ALL, D), 0.01, 0.15625, ((0, 2), (1, 4)), jnp.float32),
        "gain_first": gaussian(streams_of[8], (MATS_ALL, D), 0.003, 0.046875, ((0, 2), (1, 4)), jnp.float32),
        "gain_second": jnp.clip(jnp.exp(math.log(9.999999974752427e-07) - 4.6051702 * jax.random.uniform(streams_of[9], (MATS_ALL, D), jnp.float32) ** block_scale(streams_of[9], (MATS_ALL, D), ((0, 2), (1, 4)), -0.2, 0.2)), 9.99999993922529e-09, 9.999999974752427e-07),
    }


BETA_ONE = 0.9
BETA_TWO = 0.999
EPSILON = 1e-08
NORM_EPS = 1e-06
LEARN_RATE = 0.01
GALORE_SCALE = 0.25
WEIGHT_DECAY = 0.1

def orthogonalize(ranged):
    precision_highest = lax.Precision.HIGHEST
    squares = jnp.sum(ranged * ranged)
    current = ranged / (jnp.sqrt(squares) + NORM_EPS)
    for sweep_index in range(NS_STEPS):
        gram_matrix = jnp.dot(current.T, current, precision=precision_highest)
        current = 1.5 * current - 0.5 * jnp.dot(current, gram_matrix, precision=precision_highest)
    return current

def single_matrix(inputs):
    precision_highest = lax.Precision.HIGHEST
    gradient, weight, projector, first_moment, squared_moment, step_count = inputs
    gradient_widened = gradient.astype(jnp.float32)
    folded = jnp.dot(gradient_widened.T, projector, precision=precision_highest)
    ranged = jnp.dot(gradient_widened, folded, precision=precision_highest)
    fresh_projector = orthogonalize(ranged)
    projected = jnp.dot(fresh_projector.T, gradient_widened, precision=precision_highest)
    steps_float = step_count.astype(jnp.float32)
    new_first = BETA_ONE * first_moment + (1.0 - BETA_ONE) * projected
    new_second = BETA_TWO * squared_moment + (1.0 - BETA_TWO) * projected * projected
    direction = new_first / (1.0 - BETA_ONE ** steps_float) / (jnp.sqrt(new_second / (1.0 - BETA_TWO ** steps_float)) + EPSILON)
    update = jnp.dot(fresh_projector, direction, precision=precision_highest)
    weight_float = weight.astype(jnp.float32)
    weight_next = (weight_float - LEARN_RATE * (GALORE_SCALE * update + WEIGHT_DECAY * weight_float)).astype(jnp.bfloat16)
    return (weight_next, fresh_projector, new_first, new_second)

def reference(gradient, weight, projector, first_moment, squared_moment, step_count, norm_gains, gain_gradient, gain_first, gain_second):
    weight_next, fresh_projector, new_first, new_second = lax.map(single_matrix, (gradient, weight, projector, first_moment, squared_moment, step_count))
    steps_float = step_count.astype(jnp.float32)[:, None]
    new_gain_first = BETA_ONE * gain_first + (1.0 - BETA_ONE) * gain_gradient
    new_gain_second = BETA_TWO * gain_second + (1.0 - BETA_TWO) * gain_gradient * gain_gradient
    new_gains = norm_gains - LEARN_RATE * (new_gain_first / (1.0 - BETA_ONE ** steps_float)) / (jnp.sqrt(new_gain_second / (1.0 - BETA_TWO ** steps_float)) + EPSILON)
    return (weight_next, fresh_projector, new_first, new_second, new_gains, new_gain_first, new_gain_second)
```

```python
import functools

import jax
import jax.numpy as jnp
from jax import lax
from jax.experimental import pallas as pl
from jax.experimental.pallas import tpu as pltpu
from jax.sharding import PartitionSpec as P

NS_STEPS = 5
BETA_ONE = 0.9
BETA_TWO = 0.999
EPSILON = 1e-08
NORM_EPS = 1e-06
LEARN_RATE = 0.01
GALORE_SCALE = 0.25
WEIGHT_DECAY = 0.1


F32 = jnp.float32
BF16 = jnp.bfloat16
VMEM = pl.BlockSpec(memory_space=pltpu.VMEM)
SMEM = pl.BlockSpec(memory_space=pltpu.SMEM)


def split(x):
    hi = x.astype(BF16)
    return hi, (x - hi.astype(F32)).astype(BF16)


def dot(a, b, dims=((1,), (0,))):
    return lax.dot_general(a, b, (dims, ((), ())), preferred_element_type=F32)


def dot3(a, b, dims=((1,), (0,))):
    return dot(a[0], b[0], dims) + (dot(a[0], b[1], dims) + dot(a[1], b[0], dims))


def dot_exact_left(a, b, dims=((1,), (0,))):
    return dot(a, b[0], dims) + dot(a, b[1], dims)


def fold_kernel(gradient, projector, first, second, folded, pack):
    mats, rows, cols = gradient.shape
    own_rank = first.shape[1]
    for m in range(mats):
        g = gradient[m]
        pack[m, :rows] = g.astype(F32)
        pack[m, rows : rows + own_rank] = first[m]
        pack[m, rows + own_rank :] = second[m]
        folded[m] = dot_exact_left(g, split(projector[m]), ((0,), (0,)))


def range_kernel(gradient, f0, f1, f2, f3, ranged):
    mats, rows, cols = gradient.shape
    for m in range(mats):
        total = (f0[m] + f1[m]) + (f2[m] + f3[m])
        ranged[m * rows : (m + 1) * rows] = dot_exact_left(gradient[m], split(total))


def spread_kernel(parts, out):
    total = jnp.sum(parts[...], axis=0)
    for i in range(out.shape[0]):
        out[i] = total


def finish_kernel(
    ranged, gradient, first, second, r1, r2, r3, weight, corrections,
    weight_next, fresh, new_first, new_second,
    projected_at, direction_at,
):
    mats, rows, cols = gradient.shape
    own_rank = first.shape[1]
    tensor = r_size = 4
    rank = ranged.shape[1]
    me = lax.axis_index("tensor")
    block_rows = mats * rows
    eye = (
        lax.broadcasted_iota(jnp.int32, (rank, rank), 0)
        == lax.broadcasted_iota(jnp.int32, (rank, rank), 1)
    ).astype(F32)
    received = (None, r1, r2, r3)
    owner = [lax.rem(me + (tensor - k), tensor) for k in range(tensor)]
    state = []
    for m in range(mats):
        gram = jnp.zeros((rank, rank), F32)
        cross = jnp.zeros((rank, cols), F32)
        squares = jnp.zeros((8, rank), F32)
        for k in range(tensor):
            start = pl.multiple_of(owner[k] * block_rows + m * rows, 8)
            y = ranged[pl.ds(start, rows), :]
            ys = split(y)
            yt = (ys[0].T, ys[1].T)
            g = gradient[m] if k == 0 else received[k][m, :rows].astype(BF16)
            gram += dot3(yt, ys)
            cross += dot(yt[0], g) + dot(yt[1], g)
            squares += jnp.sum((y * y).reshape(rows // 8, 8, rank), axis=0)
            if k == 0:
                mine = y
        inverse = 1.0 / (jnp.sqrt(jnp.sum(squares)) + NORM_EPS)
        state.append([gram * (inverse * inverse), cross * inverse, mine * inverse])
    for sweep in range(NS_STEPS):
        for m in range(mats):
            gram, cross, mine = state[m]
            step = split(1.5 * eye - 0.5 * gram)
            cross = dot3(step, split(cross))
            mine = dot3(split(mine), step)
            if sweep < NS_STEPS - 1:
                gram = dot3(split(dot3(step, split(gram))), step)
            state[m] = [gram, cross, mine]
    for m in range(mats):
        _, cross, mine = state[m]
        fresh[m] = mine
        projected_at[m] = cross
        c1 = corrections[m, 0]
        c2 = corrections[m, 1]
        for k in range(tensor):
            at = pl.ds(pl.multiple_of(owner[k] * own_rank, 8), own_rank)
            projected = projected_at[m, at, :]
            if k == 0:
                m1, m2 = first[m], second[m]
            else:
                m1 = received[k][m, rows : rows + own_rank]
                m2 = received[k][m, rows + own_rank :]
            n1 = BETA_ONE * m1 + (1.0 - BETA_ONE) * projected
            n2 = BETA_TWO * m2 + (1.0 - BETA_TWO) * projected * projected
            if k == 0:
                new_first[m] = n1
                new_second[m] = n2
            direction_at[m, at, :] = n1 / c1 / (jnp.sqrt(n2 / c2) + EPSILON)
        update = dot3(split(mine), split(direction_at[m]))
        w = weight[m].astype(F32)
        weight_next[m] = (
            w - LEARN_RATE * (GALORE_SCALE * update + WEIGHT_DECAY * w)
        ).astype(BF16)


def shards(
    gradient,
    weight,
    projector,
    first_moment,
    squared_moment,
    step_count,
    norm_gains,
    gain_gradient,
    gain_first,
    gain_second,
):
    mats, rows, cols = gradient.shape
    rank = projector.shape[2]
    own_rank = first_moment.shape[1]
    tensor = lax.axis_size("tensor")
    spread = lax.axis_size("shards")
    block = mats * rows // spread
    shape = jax.ShapeDtypeStruct

    def shifted(x, k):
        return lax.ppermute(x, "tensor", [(i, (i + k) % tensor) for i in range(tensor)])

    folded, pack = pl.pallas_call(
        fold_kernel,
        out_shape=(
            shape((mats, cols, rank), F32),
            shape((mats, rows + 2 * own_rank, cols), F32),
        ),
        in_specs=[VMEM] * 4,
        out_specs=(VMEM, VMEM),
        name="fold",
    )(gradient, projector, first_moment, squared_moment)
    f1, f3, f2 = (shifted(folded, k) for k in (1, 3, 2))
    r1, r3, r2 = (shifted(pack, k) for k in (1, 3, 2))

    steps = step_count.astype(F32)[:, None]
    correct_one = 1.0 - BETA_ONE**steps
    correct_two = 1.0 - BETA_TWO**steps
    new_gain_first = BETA_ONE * gain_first + (1.0 - BETA_ONE) * gain_gradient
    new_gain_second = BETA_TWO * gain_second + (1.0 - BETA_TWO) * gain_gradient * gain_gradient
    new_gains = norm_gains - LEARN_RATE * (new_gain_first / correct_one) / (
        jnp.sqrt(new_gain_second / correct_two) + EPSILON
    )
    corrections = jnp.concatenate([correct_one, correct_two], axis=1)

    ranged_part = pl.pallas_call(
        range_kernel,
        out_shape=shape((mats * rows, rank), F32),
        in_specs=[VMEM] * 5,
        out_specs=VMEM,
        name="range",
    )(gradient, folded, f1, f2, f3)
    parts = lax.all_to_all(ranged_part, "shards", 0, 0, tiled=True)
    blocks = pl.pallas_call(
        spread_kernel,
        out_shape=shape((spread * tensor, block, rank), F32),
        in_specs=[VMEM],
        out_specs=VMEM,
        name="spread",
    )(parts.reshape(spread, block, rank))
    ranged = lax.all_to_all(
        blocks.reshape(spread * tensor * block, rank), ("tensor", "shards"), 0, 0, tiled=True
    )
    weight_next, fresh_projector, new_first, new_second = pl.pallas_call(
        finish_kernel,
        out_shape=(
            shape(weight.shape, weight.dtype),
            shape(projector.shape, F32),
            shape(first_moment.shape, F32),
            shape(squared_moment.shape, F32),
        ),
        in_specs=[VMEM] * 8 + [SMEM],
        out_specs=(VMEM,) * 4,
        scratch_shapes=[
            pltpu.VMEM((mats, rank, cols), F32),
            pltpu.VMEM((mats, rank, cols), F32),
        ],
        name="finish",
    )(ranged, gradient, first_moment, squared_moment, r1, r2, r3, weight, corrections)
    return (
        weight_next,
        fresh_projector,
        new_first,
        new_second,
        new_gains,
        new_gain_first,
        new_gain_second,
    )


def solution(mesh):
    return jax.shard_map(
        shards,
        mesh=mesh,
        in_specs=(
            P("section", "tensor", "shards"),
            P("section", "tensor", "shards"),
            P("section", "tensor", None),
            P("section", "tensor", "shards"),
            P("section", "tensor", "shards"),
            P("section"),
            P("section", "tensor"),
            P("section", "tensor"),
            P("section", "tensor"),
            P("section", "tensor"),
        ),
        out_specs=(
            P("section", "tensor", "shards"),
            P("section", "tensor", None),
            P("section", "tensor", "shards"),
            P("section", "tensor", "shards"),
            P("section", "tensor"),
            P("section", "tensor"),
            P("section", "tensor"),
        ),
        check_vma=False,
    )
```

```python
import jax
import jax.numpy as jnp
from jax import lax
from jax.experimental import pallas as pl
from jax.experimental.pallas import tpu as pltpu
from jax.sharding import PartitionSpec as P


NS_STEPS = 5
BETA_ONE = 0.9
BETA_TWO = 0.999
EPSILON = 1e-08
NORM_EPS = 1e-06
LEARN_RATE = 0.01
GALORE_SCALE = 0.25
WEIGHT_DECAY = 0.1


F32 = jnp.float32
BF16 = jnp.bfloat16
TENSOR = 4
VMEM = pl.BlockSpec(memory_space=pltpu.VMEM)
SMEM = pl.BlockSpec(memory_space=pltpu.SMEM)


def split(x):
    hi = x.astype(BF16)
    return hi, (x - hi.astype(F32)).astype(BF16)


def dot(a, b, dims=((1,), (0,))):
    return lax.dot_general(a, b, (dims, ((), ())), preferred_element_type=F32)


def dot3(a, b, dims=((1,), (0,))):
    return dot(a[0], b[0], dims) + (dot(a[0], b[1], dims) + dot(a[1], b[0], dims))


def dot_exact_left(a, b, dims=((1,), (0,))):
    return dot(a, b[0], dims) + dot(a, b[1], dims)


def fold_kernel(gradient, projector, own, s1, s2, s3):
    _, rows, _ = gradient.shape
    half = own.shape[1]
    me = lax.axis_index("tensor")
    for k, out in enumerate((own, s1, s2, s3)):
        peer = lax.rem(me + k, TENSOR)
        m, h = peer // 2, lax.rem(peer, 2)
        g = gradient[m]
        p = projector[m, :, pl.ds(pl.multiple_of(h * half, half), half)]
        f = dot_exact_left(g, split(p), ((0,), (0,)))
        if k == 0:
            out[...] = f
        else:
            out[:rows] = g.astype(F32)
            out[rows:] = f


def pack_kernel(gradient, first, second, p1, p2, p3):
    mats, rows, _ = gradient.shape
    own_rank = first.shape[1]
    me = lax.axis_index("tensor")
    for k, out in enumerate((p1, p2, p3)):
        m = lax.rem(me + k + 1, TENSOR) // 2
        out[:rows] = gradient[1 - m].astype(F32)
        for i in range(mats):
            out[rows + i * own_rank : rows + (i + 1) * own_rank] = first[i]
            at = rows + (mats + i) * own_rank
            out[at : at + own_rank] = second[i]


def range_kernel(gradient, own, r1, r2, r3, ranged):
    _, rows, _ = gradient.shape
    me = lax.axis_index("tensor")
    total = (own[...] + r1[rows:]) + (r2[rows:] + r3[rows:])
    total = split(total)
    for k, r in enumerate((None, r1, r2, r3)):
        peer = lax.rem(me + (TENSOR - k), TENSOR)
        g = gradient[me // 2] if k == 0 else r[:rows].astype(BF16)
        ranged[pl.ds(pl.multiple_of(peer * rows, 8), rows), :] = dot_exact_left(g, total)


def spread_kernel(parts, out):
    total = jnp.sum(parts[...], axis=0)
    for i in range(out.shape[0]):
        out[i] = total


def finish_kernel(
    ranged, gradient, first, second, r1, r2, r3, p1, p2, p3, weight, corrections,
    weight_next, fresh, new_first, new_second,
    projected_at, direction_at,
):
    mats, rows, cols = gradient.shape
    own_rank = first.shape[1]
    half = ranged.shape[2]
    rank = 2 * half
    me = lax.axis_index("tensor")
    eye = (
        lax.broadcasted_iota(jnp.int32, (rank, rank), 0)
        == lax.broadcasted_iota(jnp.int32, (rank, rank), 1)
    ).astype(F32)
    owner = [lax.rem(me + (TENSOR - k), TENSOR) for k in range(TENSOR)]
    which = (me // 2, 1 - me // 2)
    sides = ((None, r1, r2, r3), (None, p1, p2, p3))
    moments = (None, p1, p2, p3)
    state = []
    for m, side in zip(which, sides):
        gram = jnp.zeros((rank, rank), F32)
        cross = jnp.zeros((rank, cols), F32)
        squares = jnp.zeros((8, rank), F32)
        for k in range(TENSOR):
            at = pl.ds(pl.multiple_of(owner[k] * rows, 8), rows)
            y = jnp.concatenate([ranged[2 * m, at, :], ranged[2 * m + 1, at, :]], axis=1)
            ys = split(y)
            yt = (ys[0].T, ys[1].T)
            g = gradient[m] if k == 0 else side[k][:rows].astype(BF16)
            gram += dot3(yt, ys)
            cross += dot(yt[0], g) + dot(yt[1], g)
            squares += jnp.sum((y * y).reshape(rows // 8, 8, rank), axis=0)
            if k == 0:
                mine = y
        inverse = 1.0 / (jnp.sqrt(jnp.sum(squares)) + NORM_EPS)
        state.append([gram * (inverse * inverse), cross * inverse, mine * inverse])
    for sweep in range(NS_STEPS):
        for i in range(mats):
            gram, cross, mine = state[i]
            step = split(1.5 * eye - 0.5 * gram)
            cross = dot3(step, split(cross))
            mine = dot3(split(mine), step)
            if sweep < NS_STEPS - 1:
                gram = dot3(split(dot3(step, split(gram))), step)
            state[i] = [gram, cross, mine]
    for i, m in enumerate(which):
        _, cross, mine = state[i]
        fresh[m] = mine
        projected_at[i] = cross
        c1 = corrections[m, 0]
        c2 = corrections[m, 1]
        for k in range(TENSOR):
            at = pl.ds(pl.multiple_of(owner[k] * own_rank, 8), own_rank)
            projected = projected_at[i, at, :]
            if k == 0:
                m1, m2 = first[m], second[m]
            else:
                from_first = pl.multiple_of(rows + m * own_rank, 8)
                from_second = pl.multiple_of(rows + (mats + m) * own_rank, 8)
                m1 = moments[k][pl.ds(from_first, own_rank), :]
                m2 = moments[k][pl.ds(from_second, own_rank), :]
            n1 = BETA_ONE * m1 + (1.0 - BETA_ONE) * projected
            n2 = BETA_TWO * m2 + (1.0 - BETA_TWO) * projected * projected
            if k == 0:
                new_first[m] = n1
                new_second[m] = n2
            direction_at[i, at, :] = n1 / c1 / (jnp.sqrt(n2 / c2) + EPSILON)
        update = dot3(split(mine), split(direction_at[i]))
        w = weight[m].astype(F32)
        weight_next[m] = (
            w - LEARN_RATE * (GALORE_SCALE * update + WEIGHT_DECAY * w)
        ).astype(BF16)


def shards(
    gradient,
    weight,
    projector,
    first_moment,
    squared_moment,
    step_count,
    norm_gains,
    gain_gradient,
    gain_first,
    gain_second,
):
    mats, rows, cols = gradient.shape
    rank = projector.shape[2]
    own_rank = first_moment.shape[1]
    half = rank // 2
    spread = lax.axis_size("shards")
    block = TENSOR * rows // spread
    shape = jax.ShapeDtypeStruct

    def shifted(x, k):
        return lax.ppermute(x, "tensor", [(i, (i + k) % TENSOR) for i in range(TENSOR)])

    def call(kernel, out_shape, inputs, mib, in_specs=None, **more):
        outs = out_shape if isinstance(out_shape, tuple) else (out_shape,)
        got = pl.pallas_call(
            kernel,
            out_shape=outs,
            in_specs=in_specs or [VMEM] * len(inputs),
            out_specs=(VMEM,) * len(outs),
            compiler_params=pltpu.CompilerParams(vmem_limit_bytes=mib << 20),
            **more,
        )(*inputs)
        return got if isinstance(out_shape, tuple) else got[0]

    own, s1, s2, s3 = call(
        fold_kernel,
        (shape((cols, half), F32),) + (shape((rows + cols, half), F32),) * 3,
        (gradient, projector),
        8,
    )
    r2, r3, r1 = shifted(s2, 2), shifted(s3, 3), shifted(s1, 1)
    p1, p2, p3 = call(
        pack_kernel,
        (shape((rows + 2 * mats * own_rank, cols), F32),) * 3,
        (gradient, first_moment, squared_moment),
        8,
    )
    q2, q3, q1 = shifted(p2, 2), shifted(p3, 3), shifted(p1, 1)

    steps = step_count.astype(F32)[:, None]
    correct_one = 1.0 - BETA_ONE**steps
    correct_two = 1.0 - BETA_TWO**steps
    new_gain_first = BETA_ONE * gain_first + (1.0 - BETA_ONE) * gain_gradient
    new_gain_second = BETA_TWO * gain_second + (1.0 - BETA_TWO) * gain_gradient * gain_gradient
    new_gains = norm_gains - LEARN_RATE * (new_gain_first / correct_one) / (
        jnp.sqrt(new_gain_second / correct_two) + EPSILON
    )
    corrections = jnp.concatenate([correct_one, correct_two], axis=1)

    ranged_part = call(
        range_kernel, shape((TENSOR * rows, half), F32), (gradient, own, r1, r2, r3), 8
    )
    parts = lax.all_to_all(ranged_part, "shards", 0, 0, tiled=True)
    blocks = call(
        spread_kernel,
        shape((spread * TENSOR, block, half), F32),
        (parts.reshape(spread, block, half),),
        8,
    )
    ranged = lax.all_to_all(
        blocks.reshape(spread * TENSOR * block, half), ("tensor", "shards"), 0, 0, tiled=True
    ).reshape(TENSOR, spread * block, half)
    weight_next, fresh_projector, new_first, new_second = call(
        finish_kernel,
        (
            shape(weight.shape, weight.dtype),
            shape(projector.shape, F32),
            shape(first_moment.shape, F32),
            shape(squared_moment.shape, F32),
        ),
        (
            ranged, gradient, first_moment, squared_moment,
            r1, r2, r3, q1, q2, q3, weight, corrections,
        ),
        32,
        in_specs=[VMEM] * 11 + [SMEM],
        scratch_shapes=[pltpu.VMEM((mats, rank, cols), F32), pltpu.VMEM((mats, rank, cols), F32)],
    )
    return (
        weight_next,
        fresh_projector,
        new_first,
        new_second,
        new_gains,
        new_gain_first,
        new_gain_second,
    )


def solution(mesh):
    return jax.shard_map(
        shards,
        mesh=mesh,
        in_specs=(
            P("section", "tensor", "shards"),
            P("section", "tensor", "shards"),
            P("section", "tensor", None),
            P("section", "tensor", "shards"),
            P("section", "tensor", "shards"),
            P("section"),
            P("section", "tensor"),
            P("section", "tensor"),
            P("section", "tensor"),
            P("section", "tensor"),
        ),
        out_specs=(
            P("section", "tensor", "shards"),
            P("section", "tensor", None),
            P("section", "tensor", "shards"),
            P("section", "tensor", "shards"),
            P("section", "tensor"),
            P("section", "tensor"),
            P("section", "tensor"),
        ),
        check_vma=False,
    )
```

```python
import functools

import jax
import jax.numpy as jnp
from jax import lax
from jax.experimental import pallas as pl
from jax.experimental.pallas import tpu as pltpu
from jax.sharding import PartitionSpec as P


NS_STEPS = 5
BETA_ONE = 0.9
BETA_TWO = 0.999
EPSILON = 1e-08
NORM_EPS = 1e-06
LEARN_RATE = 0.01
GALORE_SCALE = 0.25
WEIGHT_DECAY = 0.1


F32 = jnp.float32
BF16 = jnp.bfloat16
TENSOR = 4
VMEM = pl.BlockSpec(memory_space=pltpu.VMEM)
SMEM = pl.BlockSpec(memory_space=pltpu.SMEM)


def split(x):
    hi = x.astype(BF16)
    return hi, (x - hi.astype(F32)).astype(BF16)


def dot(a, b, dims=((1,), (0,))):
    return lax.dot_general(a, b, (dims, ((), ())), preferred_element_type=F32)


def dot3(a, b, dims=((1,), (0,))):
    return dot(a[0], b[0], dims) + (dot(a[0], b[1], dims) + dot(a[1], b[0], dims))


def dot_exact_left(a, b, dims=((1,), (0,))):
    return dot(a, b[0], dims) + dot(a, b[1], dims)


def fold_kernel(gradient, projector, own, s1, s2, s3):
    _, rows, _ = gradient.shape
    half = own.shape[1]
    me = lax.axis_index("tensor")
    for k, out in enumerate((own, s1, s2, s3)):
        peer = lax.rem(me + k, TENSOR)
        m, h = peer // 2, lax.rem(peer, 2)
        g = gradient[m]
        p = projector[m, :, pl.ds(pl.multiple_of(h * half, half), half)]
        f = dot_exact_left(g, split(p), ((0,), (0,)))
        if k == 0:
            out[...] = f
        else:
            out[:rows] = g.astype(F32)
            out[rows:] = f


def corrections(steps, m):
    one = jnp.float32(1.0)
    powers = lax.fori_loop(
        0, steps[m], lambda _, p: (p[0] * jnp.float32(BETA_ONE), p[1] * jnp.float32(BETA_TWO)), (one, one)
    )
    return 1.0 - powers[0], 1.0 - powers[1]


def pack_kernel(
    steps, first, second, gains, gain_gradient, gain_first, gain_second,
    pack, new_gains, new_gain_first, new_gain_second,
):
    mats, own_rank, _ = first.shape
    for i in range(mats):
        pack[i * own_rank : (i + 1) * own_rank] = first[i]
        pack[(mats + i) * own_rank : (mats + i + 1) * own_rank] = second[i]
    for i in range(mats):
        c1, c2 = corrections(steps, i)
        row = slice(i, i + 1)
        g = gain_gradient[row]
        n1 = BETA_ONE * gain_first[row] + (1.0 - BETA_ONE) * g
        n2 = BETA_TWO * gain_second[row] + (1.0 - BETA_TWO) * g * g
        new_gain_first[row] = n1
        new_gain_second[row] = n2
        new_gains[row] = gains[row] - LEARN_RATE * (n1 / c1) / (jnp.sqrt(n2 / c2) + EPSILON)


def range_kernel(gradient, own, r1, r2, r3, ranged):
    _, rows, _ = gradient.shape
    me = lax.axis_index("tensor")
    total = (own[...] + r1[rows:]) + (r2[rows:] + r3[rows:])
    total = split(total)
    for k, r in enumerate((None, r1, r2, r3)):
        peer = lax.rem(me + (TENSOR - k), TENSOR)
        g = gradient[me // 2] if k == 0 else r[:rows].astype(BF16)
        ranged[pl.ds(pl.multiple_of(peer * rows, 8), rows), :] = dot_exact_left(g, total)


def spread_kernel(parts, out):
    total = jnp.sum(parts[...], axis=0)
    for i in range(out.shape[0]):
        out[i] = total


def own_rows(gradient, r1, r2, r3):
    rows = gradient.shape[1]
    me = lax.axis_index("tensor")
    for k, r in enumerate((None, r1, r2, r3)):
        start = pl.multiple_of(lax.rem(me + (TENSOR - k), TENSOR) * rows, 8)
        yield start, gradient[me // 2] if k == 0 else r[:rows].astype(BF16)


def own_products_kernel(mine, gradient, r1, r2, r3, to_across, to_opposite):
    rows = gradient.shape[1]
    half = mine.shape[1]
    me = lax.axis_index("tensor")
    gram = jnp.zeros((half, half), F32)
    cross = jnp.zeros((half, gradient.shape[2]), F32)
    for start, g in own_rows(gradient, r1, r2, r3):
        ys = split(mine[pl.ds(start, rows), :])
        yt = (ys[0].T, ys[1].T)
        gram += dot3(yt, ys)
        cross += dot(yt[0], g) + dot(yt[1], g)
    for mask, out in ((3, to_across), (2, to_opposite)):
        peer = me ^ mask
        out[:half] = cross
        out[half : 2 * half] = gram
        out[2 * half :] = mine[pl.ds(pl.multiple_of(peer * rows, 8), rows), :]


def joint_products_kernel(mine, beside, gradient, r1, r2, r3, joint, near):
    rows = gradient.shape[1]
    half = mine.shape[1]
    between = jnp.zeros((half, half), F32)
    gram = jnp.zeros((half, half), F32)
    cross = jnp.zeros((half, gradient.shape[2]), F32)
    for start, g in own_rows(gradient, r1, r2, r3):
        at = pl.ds(start, rows)
        xs, ys = split(mine[at, :]), split(beside[at, :])
        xt, yt = (xs[0].T, xs[1].T), (ys[0].T, ys[1].T)
        between += dot3(xt, ys)
        gram += dot3(yt, ys)
        cross += dot(yt[0], g) + dot(yt[1], g)
    joint[...] = between
    near[:half] = cross
    near[half : 2 * half] = gram
    me = lax.axis_index("tensor")
    near[2 * half :] = beside[pl.ds(pl.multiple_of(me * rows, 8), rows), :]


def finish_kernel(
    other, same, swap, joint, first, second, weight, q1, q2, q3, steps, *rest,
):
    rest = list(rest)
    basis = None if other else rest.pop(0)
    earlier, outs = rest[:-8], rest[-8:-4]
    grams, crosses, direction_at, locals_ = rest[-4:]
    weight_next, fresh, new_first, new_second = outs
    mats, own_rank, _ = first.shape
    rows = weight.shape[1]
    half = joint.shape[1]
    rank = 2 * half
    me = lax.axis_index("tensor")
    mine = me // 2
    m = 1 - mine if other else mine
    h = lax.rem(me, 2)
    if earlier:
        for before, out in zip(earlier, outs):
            out[mine] = before[...]
        put = lambda ref, value: ref.__setitem__(m, value)
    else:
        put = lambda ref, value: ref.__setitem__(Ellipsis, value)
    here = pl.ds(pl.multiple_of(h * half, half), half)
    there = pl.ds(pl.multiple_of((1 - h) * half, half), half)
    grams[here, here] = same[half : 2 * half]
    grams[there, there] = swap[half : 2 * half]
    between = joint[...]
    if other:
        grams[there, here] = between
        grams[here, there] = between.T
        locals_[:, here] = same[2 * half :]
    else:
        grams[here, there] = between
        grams[there, here] = between.T
        locals_[:, here] = basis[pl.ds(pl.multiple_of(me * rows, 8), rows), :]
    locals_[:, there] = swap[2 * half :]
    crosses[here, :] = same[:half]
    crosses[there, :] = swap[:half]
    eye = (
        lax.broadcasted_iota(jnp.int32, (rank, rank), 0)
        == lax.broadcasted_iota(jnp.int32, (rank, rank), 1)
    ).astype(F32)
    gram = grams[...]
    inverse = 1.0 / (jnp.sqrt(jnp.sum(gram * eye)) + NORM_EPS)
    gram, cross, local = gram * (inverse * inverse), crosses[...] * inverse, locals_[...] * inverse
    for sweep in range(NS_STEPS):
        step = split(1.5 * eye - 0.5 * gram)
        cross = dot3(step, split(cross))
        local = dot3(split(local), step)
        if sweep < NS_STEPS - 1:
            gram = dot3(split(dot3(step, split(gram))), step)
    put(fresh, local)
    crosses[...] = cross
    c1, c2 = corrections(steps, m)
    for k, q in enumerate((None, q1, q2, q3)):
        peer = lax.rem(me + (TENSOR - k), TENSOR)
        at = pl.ds(pl.multiple_of(peer * own_rank, 8), own_rank)
        projected = crosses[at, :]
        if k == 0:
            m1, m2 = first[m], second[m]
        else:
            m1 = q[pl.ds(pl.multiple_of(m * own_rank, 8), own_rank), :]
            m2 = q[pl.ds(pl.multiple_of((mats + m) * own_rank, 8), own_rank), :]
        n1 = BETA_ONE * m1 + (1.0 - BETA_ONE) * projected
        n2 = BETA_TWO * m2 + (1.0 - BETA_TWO) * projected * projected
        if k == 0:
            put(new_first, n1)
            put(new_second, n2)
        direction_at[at, :] = n1 / c1 / (jnp.sqrt(n2 / c2) + EPSILON)
    update = dot3(split(local), split(direction_at[...]))
    w = weight[m].astype(F32)
    put(weight_next, (w - LEARN_RATE * (GALORE_SCALE * update + WEIGHT_DECAY * w)).astype(BF16))


def shards(
    gradient,
    weight,
    projector,
    first_moment,
    squared_moment,
    step_count,
    norm_gains,
    gain_gradient,
    gain_first,
    gain_second,
):
    mats, rows, cols = gradient.shape
    rank = projector.shape[2]
    own_rank = first_moment.shape[1]
    half = rank // 2
    spread = lax.axis_size("shards")
    block = TENSOR * rows // spread
    shape = jax.ShapeDtypeStruct

    def shifted(x, k):
        return lax.ppermute(x, "tensor", [(i, (i + k) % TENSOR) for i in range(TENSOR)])

    def swapped(x, mask):
        return lax.ppermute(x, "tensor", [(i, i ^ mask) for i in range(TENSOR)])

    def call(kernel, out_shape, inputs, mib, in_specs=None, **more):
        outs = out_shape if isinstance(out_shape, tuple) else (out_shape,)
        got = pl.pallas_call(
            kernel,
            out_shape=outs,
            in_specs=in_specs or [VMEM] * len(inputs),
            out_specs=(VMEM,) * len(outs),
            compiler_params=pltpu.CompilerParams(vmem_limit_bytes=mib << 20),
            **more,
        )(*inputs)
        return got if isinstance(out_shape, tuple) else got[0]

    own, s1, s2, s3 = call(
        fold_kernel,
        (shape((cols, half), F32),) + (shape((rows + cols, half), F32),) * 3,
        (gradient, projector),
        8,
    )
    r2, r3, r1 = shifted(s2, 2), shifted(s3, 3), shifted(s1, 1)
    small = shape(norm_gains.shape, F32)
    pack, new_gains, new_gain_first, new_gain_second = call(
        pack_kernel,
        (shape((2 * mats * own_rank, cols), F32),) + (small,) * 3,
        (
            step_count, first_moment, squared_moment,
            norm_gains, gain_gradient, gain_first, gain_second,
        ),
        8,
        in_specs=[SMEM] + [VMEM] * 6,
    )
    q2, q3, q1 = shifted(pack, 2), shifted(pack, 3), shifted(pack, 1)

    ranged_part = call(
        range_kernel, shape((TENSOR * rows, half), F32), (gradient, own, r1, r2, r3), 8
    )
    parts = lax.all_to_all(ranged_part, "shards", 0, 0, tiled=True)
    blocks = call(
        spread_kernel, shape((spread, block, half), F32), (parts.reshape(spread, block, half),), 8
    )
    mine = lax.all_to_all(
        blocks.reshape(spread * block, half), "shards", 0, 0, tiled=True
    )
    gradients = (gradient, r1, r2, r3)
    message = shape((2 * half + rows, half), F32)
    beside = swapped(mine, 1)
    to_across, to_opposite = call(own_products_kernel, (message,) * 2, (mine,) + gradients, 8)
    across, opposite = swapped(to_across, 3), swapped(to_opposite, 2)
    joint, near = call(
        joint_products_kernel, (shape((half, half), F32), message), (mine, beside) + gradients, 8
    )
    joint_across = swapped(joint, 3)
    shapes = [weight, projector, first_moment, squared_moment]
    scratch = [
        pltpu.VMEM((rank, rank), F32),
        pltpu.VMEM((rank, cols), F32),
        pltpu.VMEM((rank, cols), F32),
        pltpu.VMEM((rows, rank), F32),
    ]
    shared = (first_moment, squared_moment, weight, q1, q2, q3, step_count)
    specs = [VMEM] * 9 + [SMEM]
    done = call(
        functools.partial(finish_kernel, False),
        tuple(shape(x.shape[1:], x.dtype) for x in shapes),
        (to_across, near, joint) + shared + (mine,),
        16,
        in_specs=specs + [VMEM],
        scratch_shapes=scratch,
    )
    weight_next, fresh_projector, new_first, new_second = call(
        functools.partial(finish_kernel, True),
        tuple(shape(x.shape, x.dtype) for x in shapes),
        (opposite, across, joint_across) + shared + done,
        16,
        in_specs=specs + [VMEM] * 4,
        scratch_shapes=scratch,
    )
    return (
        weight_next,
        fresh_projector,
        new_first,
        new_second,
        new_gains,
        new_gain_first,
        new_gain_second,
    )


def solution(mesh):
    return jax.shard_map(
        shards,
        mesh=mesh,
        in_specs=(
            P("section", "tensor", "shards"),
            P("section", "tensor", "shards"),
            P("section", "tensor", None),
            P("section", "tensor", "shards"),
            P("section", "tensor", "shards"),
            P("section"),
            P("section", "tensor"),
            P("section", "tensor"),
            P("section", "tensor"),
            P("section", "tensor"),
        ),
        out_specs=(
            P("section", "tensor", "shards"),
            P("section", "tensor", None),
            P("section", "tensor", "shards"),
            P("section", "tensor", "shards"),
            P("section", "tensor"),
            P("section", "tensor"),
            P("section", "tensor"),
        ),
        check_vma=False,
    )
```

```python
import jax
import jax.numpy as jnp
from jax import lax
from jax.experimental import pallas as pl
from jax.experimental.pallas import tpu as pltpu
from jax.sharding import PartitionSpec as P


NS_STEPS = 5
BETA_ONE = 0.9
BETA_TWO = 0.999
EPSILON = 1e-08
NORM_EPS = 1e-06
LEARN_RATE = 0.01
GALORE_SCALE = 0.25
WEIGHT_DECAY = 0.1


F32 = jnp.float32
BF16 = jnp.bfloat16
TENSOR = 4
VMEM = pl.BlockSpec(memory_space=pltpu.VMEM)
SMEM = pl.BlockSpec(memory_space=pltpu.SMEM)


def split(x):
    hi = x.astype(BF16)
    return hi, (x - hi.astype(F32)).astype(BF16)


def dot(a, b, dims=((1,), (0,))):
    return lax.dot_general(a, b, (dims, ((), ())), preferred_element_type=F32)


def dot3(a, b, dims=((1,), (0,))):
    return dot(a[0], b[0], dims) + (dot(a[0], b[1], dims) + dot(a[1], b[0], dims))


def dot_exact_left(a, b, dims=((1,), (0,))):
    return dot(a, b[0], dims) + dot(a, b[1], dims)


def fold_kernel(gradient, projector, own, s1, s2, s3):
    _, rows, _ = gradient.shape
    half = own.shape[1]
    me = lax.axis_index("tensor")
    for k, out in enumerate((own, s1, s2, s3)):
        peer = lax.rem(me + k, TENSOR)
        m, h = peer // 2, lax.rem(peer, 2)
        g = gradient[m]
        p = projector[m, :, pl.ds(pl.multiple_of(h * half, half), half)]
        f = dot_exact_left(g, split(p), ((0,), (0,)))
        if k == 0:
            out[...] = f
        else:
            out[:rows] = g.astype(F32)
            out[rows:] = f


def corrections(steps, m):
    one = jnp.float32(1.0)
    powers = lax.fori_loop(
        0, steps[m], lambda _, p: (p[0] * jnp.float32(BETA_ONE), p[1] * jnp.float32(BETA_TWO)), (one, one)
    )
    return 1.0 - powers[0], 1.0 - powers[1]


def pack_kernel(
    steps, first, second, gains, gain_gradient, gain_first, gain_second,
    pack, new_gains, new_gain_first, new_gain_second,
):
    mats, own_rank, _ = first.shape
    for i in range(mats):
        pack[i * own_rank : (i + 1) * own_rank] = first[i]
        pack[(mats + i) * own_rank : (mats + i + 1) * own_rank] = second[i]
    for i in range(mats):
        c1, c2 = corrections(steps, i)
        row = slice(i, i + 1)
        g = gain_gradient[row]
        n1 = BETA_ONE * gain_first[row] + (1.0 - BETA_ONE) * g
        n2 = BETA_TWO * gain_second[row] + (1.0 - BETA_TWO) * g * g
        new_gain_first[row] = n1
        new_gain_second[row] = n2
        new_gains[row] = gains[row] - LEARN_RATE * (n1 / c1) / (jnp.sqrt(n2 / c2) + EPSILON)


def range_kernel(gradient, own, r1, r2, r3, ranged):
    _, rows, _ = gradient.shape
    me = lax.axis_index("tensor")
    total = (own[...] + r1[rows:]) + (r2[rows:] + r3[rows:])
    total = split(total)
    for k, r in enumerate((None, r1, r2, r3)):
        peer = lax.rem(me + (TENSOR - k), TENSOR)
        g = gradient[me // 2] if k == 0 else r[:rows].astype(BF16)
        ranged[pl.ds(pl.multiple_of(peer * rows, 8), rows), :] = dot_exact_left(g, total)


def spread_kernel(parts, out):
    total = jnp.sum(parts[...], axis=0)
    for i in range(out.shape[0]):
        out[i] = total


def own_rows(gradient, r1, r2, r3):
    rows = gradient.shape[1]
    me = lax.axis_index("tensor")
    for k, r in enumerate((None, r1, r2, r3)):
        start = pl.multiple_of(lax.rem(me + (TENSOR - k), TENSOR) * rows, 8)
        yield start, gradient[me // 2] if k == 0 else r[:rows].astype(BF16)


def own_products_kernel(mine, gradient, r1, r2, r3, to_across, to_opposite):
    rows = gradient.shape[1]
    half = mine.shape[1]
    me = lax.axis_index("tensor")
    gram = jnp.zeros((half, half), F32)
    cross = jnp.zeros((half, gradient.shape[2]), F32)
    for start, g in own_rows(gradient, r1, r2, r3):
        ys = split(mine[pl.ds(start, rows), :])
        yt = (ys[0].T, ys[1].T)
        gram += dot3(yt, ys)
        cross += dot(yt[0], g) + dot(yt[1], g)
    for mask, out in ((3, to_across), (2, to_opposite)):
        peer = me ^ mask
        out[:half] = cross
        out[half : 2 * half] = gram
        out[2 * half :] = mine[pl.ds(pl.multiple_of(peer * rows, 8), rows), :]


def joint_products_kernel(mine, beside, gradient, r1, r2, r3, joint, near):
    rows = gradient.shape[1]
    half = mine.shape[1]
    between = jnp.zeros((half, half), F32)
    gram = jnp.zeros((half, half), F32)
    cross = jnp.zeros((half, gradient.shape[2]), F32)
    for start, g in own_rows(gradient, r1, r2, r3):
        at = pl.ds(start, rows)
        xs, ys = split(mine[at, :]), split(beside[at, :])
        xt, yt = (xs[0].T, xs[1].T), (ys[0].T, ys[1].T)
        between += dot3(xt, ys)
        gram += dot3(yt, ys)
        cross += dot(yt[0], g) + dot(yt[1], g)
    joint[...] = between
    near[:half] = cross
    near[half : 2 * half] = gram
    me = lax.axis_index("tensor")
    near[2 * half :] = beside[pl.ds(pl.multiple_of(me * rows, 8), rows), :]


def finish_kernel(
    same_mine, swap_mine, joint_mine, same_other, swap_other, joint_other, basis,
    first, second, weight, q1, q2, q3, steps,
    weight_next, fresh, new_first, new_second,
    grams, crosses, directions, locals_,
):
    mats, own_rank, _ = first.shape
    rows = weight.shape[1]
    half = joint_mine.shape[1]
    rank = 2 * half
    me = lax.axis_index("tensor")
    h = lax.rem(me, 2)
    here = pl.ds(pl.multiple_of(h * half, half), half)
    there = pl.ds(pl.multiple_of((1 - h) * half, half), half)
    eye = (
        lax.broadcasted_iota(jnp.int32, (rank, rank), 0)
        == lax.broadcasted_iota(jnp.int32, (rank, rank), 1)
    ).astype(F32)
    which = (me // 2, 1 - me // 2)
    state = []
    for i, (same, swap, joint) in enumerate(
        ((same_mine, swap_mine, joint_mine), (same_other, swap_other, joint_other))
    ):
        grams[i, here, here] = same[half : 2 * half]
        grams[i, there, there] = swap[half : 2 * half]
        between = joint[...]
        if i == 0:
            grams[i, here, there] = between
            grams[i, there, here] = between.T
            locals_[i, :, here] = basis[pl.ds(pl.multiple_of(me * rows, 8), rows), :]
        else:
            grams[i, there, here] = between
            grams[i, here, there] = between.T
            locals_[i, :, here] = same[2 * half :]
        locals_[i, :, there] = swap[2 * half :]
        crosses[i, here, :] = same[:half]
        crosses[i, there, :] = swap[:half]
        gram = grams[i]
        inverse = 1.0 / (jnp.sqrt(jnp.sum(gram * eye)) + NORM_EPS)
        state.append((gram * (inverse * inverse), crosses[i] * inverse, locals_[i] * inverse))
    for sweep in range(NS_STEPS):
        steps_ = [split(1.5 * eye - 0.5 * gram) for gram, _, _ in state]
        if sweep < NS_STEPS - 1:
            halfway = [split(dot3(p, split(s[0]))) for p, s in zip(steps_, state)]
            grams_ = [dot3(x, p) for x, p in zip(halfway, steps_)]
        else:
            grams_ = [None] * mats
        state = [
            (gram, dot3(p, split(s[1])), dot3(split(s[2]), p))
            for gram, p, s in zip(grams_, steps_, state)
        ]
    for i, m in enumerate(which):
        _, cross, local = state[i]
        fresh[m] = local
        crosses[i] = cross
        c1, c2 = corrections(steps, m)
        for k, q in enumerate((None, q1, q2, q3)):
            peer = lax.rem(me + (TENSOR - k), TENSOR)
            at = pl.ds(pl.multiple_of(peer * own_rank, 8), own_rank)
            projected = crosses[i, at, :]
            if k == 0:
                m1, m2 = first[m], second[m]
            else:
                m1 = q[pl.ds(pl.multiple_of(m * own_rank, 8), own_rank), :]
                m2 = q[pl.ds(pl.multiple_of((mats + m) * own_rank, 8), own_rank), :]
            n1 = BETA_ONE * m1 + (1.0 - BETA_ONE) * projected
            n2 = BETA_TWO * m2 + (1.0 - BETA_TWO) * projected * projected
            if k == 0:
                new_first[m] = n1
                new_second[m] = n2
            directions[i, at, :] = n1 / c1 / (jnp.sqrt(n2 / c2) + EPSILON)
    for i, m in enumerate(which):
        update = dot3(split(state[i][2]), split(directions[i]))
        w = weight[m].astype(F32)
        weight_next[m] = (
            w - LEARN_RATE * (GALORE_SCALE * update + WEIGHT_DECAY * w)
        ).astype(BF16)


def shards(
    gradient,
    weight,
    projector,
    first_moment,
    squared_moment,
    step_count,
    norm_gains,
    gain_gradient,
    gain_first,
    gain_second,
):
    mats, rows, cols = gradient.shape
    rank = projector.shape[2]
    own_rank = first_moment.shape[1]
    half = rank // 2
    spread = lax.axis_size("shards")
    block = TENSOR * rows // spread
    shape = jax.ShapeDtypeStruct

    def shifted(x, k):
        return lax.ppermute(x, "tensor", [(i, (i + k) % TENSOR) for i in range(TENSOR)])

    def swapped(x, mask):
        return lax.ppermute(x, "tensor", [(i, i ^ mask) for i in range(TENSOR)])

    def call(kernel, out_shape, inputs, mib, in_specs=None, **more):
        outs = out_shape if isinstance(out_shape, tuple) else (out_shape,)
        got = pl.pallas_call(
            kernel,
            out_shape=outs,
            in_specs=in_specs or [VMEM] * len(inputs),
            out_specs=(VMEM,) * len(outs),
            compiler_params=pltpu.CompilerParams(vmem_limit_bytes=mib << 20),
            **more,
        )(*inputs)
        return got if isinstance(out_shape, tuple) else got[0]

    own, s1, s2, s3 = call(
        fold_kernel,
        (shape((cols, half), F32),) + (shape((rows + cols, half), F32),) * 3,
        (gradient, projector),
        8,
    )
    r2, r3, r1 = shifted(s2, 2), shifted(s3, 3), shifted(s1, 1)
    small = shape(norm_gains.shape, F32)
    pack, new_gains, new_gain_first, new_gain_second = call(
        pack_kernel,
        (shape((2 * mats * own_rank, cols), F32),) + (small,) * 3,
        (
            step_count, first_moment, squared_moment,
            norm_gains, gain_gradient, gain_first, gain_second,
        ),
        8,
        in_specs=[SMEM] + [VMEM] * 6,
    )
    q2, q3, q1 = shifted(pack, 2), shifted(pack, 3), shifted(pack, 1)

    ranged_part = call(
        range_kernel, shape((TENSOR * rows, half), F32), (gradient, own, r1, r2, r3), 8
    )
    parts = lax.all_to_all(ranged_part, "shards", 0, 0, tiled=True)
    blocks = call(
        spread_kernel, shape((spread, block, half), F32), (parts.reshape(spread, block, half),), 8
    )
    mine = lax.all_to_all(
        blocks.reshape(spread * block, half), "shards", 0, 0, tiled=True
    )
    gradients = (gradient, r1, r2, r3)
    message = shape((2 * half + rows, half), F32)
    beside = swapped(mine, 1)
    to_across, to_opposite = call(own_products_kernel, (message,) * 2, (mine,) + gradients, 8)
    across, opposite = swapped(to_across, 3), swapped(to_opposite, 2)
    joint, near = call(
        joint_products_kernel, (shape((half, half), F32), message), (mine, beside) + gradients, 8
    )
    joint_across = swapped(joint, 3)
    shapes = [weight, projector, first_moment, squared_moment]
    weight_next, fresh_projector, new_first, new_second = call(
        finish_kernel,
        tuple(shape(x.shape, x.dtype) for x in shapes),
        (
            to_across, near, joint, opposite, across, joint_across, mine,
            first_moment, squared_moment, weight, q1, q2, q3, step_count,
        ),
        24,
        in_specs=[VMEM] * 13 + [SMEM],
        scratch_shapes=[
            pltpu.VMEM((mats, rank, rank), F32),
            pltpu.VMEM((mats, rank, cols), F32),
            pltpu.VMEM((mats, rank, cols), F32),
            pltpu.VMEM((mats, rows, rank), F32),
        ],
    )
    return (
        weight_next,
        fresh_projector,
        new_first,
        new_second,
        new_gains,
        new_gain_first,
        new_gain_second,
    )


def solution(mesh):
    return jax.shard_map(
        shards,
        mesh=mesh,
        in_specs=(
            P("section", "tensor", "shards"),
            P("section", "tensor", "shards"),
            P("section", "tensor", None),
            P("section", "tensor", "shards"),
            P("section", "tensor", "shards"),
            P("section"),
            P("section", "tensor"),
            P("section", "tensor"),
            P("section", "tensor"),
            P("section", "tensor"),
        ),
        out_specs=(
            P("section", "tensor", "shards"),
            P("section", "tensor", None),
            P("section", "tensor", "shards"),
            P("section", "tensor", "shards"),
            P("section", "tensor"),
            P("section", "tensor"),
            P("section", "tensor"),
        ),
        check_vma=False,
    )
```

```python
import jax
import jax.numpy as jnp
from jax import lax
from jax.experimental import pallas as pl
from jax.experimental.pallas import tpu as pltpu
from jax.sharding import PartitionSpec as P


NS_STEPS = 5
BETA_ONE = 0.9
BETA_TWO = 0.999
EPSILON = 1e-08
NORM_EPS = 1e-06
LEARN_RATE = 0.01
GALORE_SCALE = 0.25
WEIGHT_DECAY = 0.1


F32 = jnp.float32
BF16 = jnp.bfloat16
TENSOR = 4
VMEM = pl.BlockSpec(memory_space=pltpu.VMEM)
SMEM = pl.BlockSpec(memory_space=pltpu.SMEM)


def split(x):
    hi = x.astype(BF16)
    return hi, (x - hi.astype(F32)).astype(BF16)


def dot(a, b, dims=((1,), (0,))):
    return lax.dot_general(a, b, (dims, ((), ())), preferred_element_type=F32)


def dot3(a, b, dims=((1,), (0,))):
    return dot(a[0], b[0], dims) + (dot(a[0], b[1], dims) + dot(a[1], b[0], dims))


def dot_exact_left(a, b, dims=((1,), (0,))):
    return dot(a, b[0], dims) + dot(a, b[1], dims)


def fold_kernel(gradient, projector, own, s1, s2, s3):
    _, rows, _ = gradient.shape
    half = own.shape[1]
    me = lax.axis_index("tensor")
    for k, out in enumerate((own, s1, s2, s3)):
        peer = lax.rem(me + k, TENSOR)
        m, h = peer // 2, lax.rem(peer, 2)
        g = gradient[m]
        p = projector[m, :, pl.ds(pl.multiple_of(h * half, half), half)]
        f = dot_exact_left(g, split(p), ((0,), (0,)))
        if k == 0:
            out[...] = f
        else:
            out[:rows] = g.astype(F32)
            out[rows:] = f


def corrections(steps, m):
    one = jnp.float32(1.0)
    powers = lax.fori_loop(
        0, steps[m], lambda _, p: (p[0] * jnp.float32(BETA_ONE), p[1] * jnp.float32(BETA_TWO)), (one, one)
    )
    return 1.0 - powers[0], 1.0 - powers[1]


def pack_kernel(
    steps, first, second, gains, gain_gradient, gain_first, gain_second,
    pack, new_gains, new_gain_first, new_gain_second,
):
    mats, own_rank, _ = first.shape
    for i in range(mats):
        pack[i * own_rank : (i + 1) * own_rank] = first[i]
        pack[(mats + i) * own_rank : (mats + i + 1) * own_rank] = second[i]
    for i in range(mats):
        c1, c2 = corrections(steps, i)
        row = slice(i, i + 1)
        g = gain_gradient[row]
        n1 = BETA_ONE * gain_first[row] + (1.0 - BETA_ONE) * g
        n2 = BETA_TWO * gain_second[row] + (1.0 - BETA_TWO) * g * g
        new_gain_first[row] = n1
        new_gain_second[row] = n2
        new_gains[row] = gains[row] - LEARN_RATE * (n1 / c1) / (jnp.sqrt(n2 / c2) + EPSILON)


def range_kernel(gradient, own, r1, r2, r3, ranged):
    _, rows, _ = gradient.shape
    me = lax.axis_index("tensor")
    total = (own[...] + r1[rows:]) + (r2[rows:] + r3[rows:])
    total = split(total)
    for k, r in enumerate((None, r1, r2, r3)):
        peer = lax.rem(me + (TENSOR - k), TENSOR)
        g = gradient[me // 2] if k == 0 else r[:rows].astype(BF16)
        ranged[pl.ds(pl.multiple_of(peer * rows, 8), rows), :] = dot_exact_left(g, total)


def spread_kernel(parts, out):
    total = jnp.sum(parts[...], axis=0)
    for i in range(out.shape[0]):
        out[i] = total


def own_rows(gradient, r1, r2, r3):
    rows = gradient.shape[1]
    me = lax.axis_index("tensor")
    for k, r in enumerate((None, r1, r2, r3)):
        start = pl.multiple_of(lax.rem(me + (TENSOR - k), TENSOR) * rows, 8)
        yield start, gradient[me // 2] if k == 0 else r[:rows].astype(BF16)


def own_products_kernel(mine, gradient, r1, r2, r3, to_across, to_opposite):
    rows = gradient.shape[1]
    half = mine.shape[1]
    me = lax.axis_index("tensor")
    gram = jnp.zeros((half, half), F32)
    cross = jnp.zeros((half, gradient.shape[2]), F32)
    for start, g in own_rows(gradient, r1, r2, r3):
        ys = split(mine[pl.ds(start, rows), :])
        yt = (ys[0].T, ys[1].T)
        gram += dot3(yt, ys)
        cross += dot(yt[0], g) + dot(yt[1], g)
    for mask, out in ((3, to_across), (2, to_opposite)):
        peer = me ^ mask
        out[:half] = cross
        out[half : 2 * half] = gram
        out[2 * half :] = mine[pl.ds(pl.multiple_of(peer * rows, 8), rows), :]


def joint_products_kernel(mine, beside, gradient, r1, r2, r3, joint, near):
    rows = gradient.shape[1]
    half = mine.shape[1]
    between = jnp.zeros((half, half), F32)
    gram = jnp.zeros((half, half), F32)
    cross = jnp.zeros((half, gradient.shape[2]), F32)
    for start, g in own_rows(gradient, r1, r2, r3):
        at = pl.ds(start, rows)
        xs, ys = split(mine[at, :]), split(beside[at, :])
        xt, yt = (xs[0].T, xs[1].T), (ys[0].T, ys[1].T)
        between += dot3(xt, ys)
        gram += dot3(yt, ys)
        cross += dot(yt[0], g) + dot(yt[1], g)
    joint[...] = between
    near[:half] = cross
    near[half : 2 * half] = gram
    me = lax.axis_index("tensor")
    near[2 * half :] = beside[pl.ds(pl.multiple_of(me * rows, 8), rows), :]


def orthogonalize(own, same, swap, joint, here_rows, grams, crosses, locals_):
    half = joint.shape[1]
    rank = 2 * half
    h = lax.rem(lax.axis_index("tensor"), 2)
    here = pl.ds(pl.multiple_of(h * half, half), half)
    there = pl.ds(pl.multiple_of((1 - h) * half, half), half)
    eye = (
        lax.broadcasted_iota(jnp.int32, (rank, rank), 0)
        == lax.broadcasted_iota(jnp.int32, (rank, rank), 1)
    ).astype(F32)
    grams[here, here] = same[half : 2 * half]
    grams[there, there] = swap[half : 2 * half]
    between = joint[...]
    first, second = (here, there) if own else (there, here)
    grams[first, second] = between
    grams[second, first] = between.T
    locals_[:, here] = here_rows
    locals_[:, there] = swap[2 * half :]
    crosses[here, :] = same[:half]
    crosses[there, :] = swap[:half]
    gram = grams[...]
    inverse = 1.0 / (jnp.sqrt(jnp.sum(gram * eye)) + NORM_EPS)
    gram, cross, local = gram * (inverse * inverse), crosses[...] * inverse, locals_[...] * inverse
    for sweep in range(NS_STEPS):
        step = split(1.5 * eye - 0.5 * gram)
        cross = dot3(step, split(cross))
        local = dot3(split(local), step)
        if sweep < NS_STEPS - 1:
            gram = dot3(split(dot3(step, split(gram))), step)
    return cross, local


def own_basis_kernel(same, swap, joint, basis, cross, local, grams, crosses, locals_):
    rows = local.shape[0]
    me = lax.axis_index("tensor")
    here_rows = basis[pl.ds(pl.multiple_of(me * rows, 8), rows), :]
    cross[...], local[...] = orthogonalize(
        True, same, swap, joint, here_rows, grams, crosses, locals_
    )


def finish_kernel(
    own_cross, own_local, same_other, swap_other, joint_other,
    first, second, weight, q1, q2, q3, steps,
    weight_next, fresh, new_first, new_second,
    crosses, directions, grams, other_crosses, locals_,
):
    mats, own_rank, _ = first.shape
    half = joint_other.shape[1]
    me = lax.axis_index("tensor")
    which = (me // 2, 1 - me // 2)
    other = orthogonalize(
        False, same_other, swap_other, joint_other, same_other[2 * half :],
        grams, other_crosses, locals_,
    )
    state = [(None, own_cross[...], own_local[...]), (None,) + other]
    for i, m in enumerate(which):
        _, cross, local = state[i]
        fresh[m] = local
        crosses[i] = cross
        c1, c2 = corrections(steps, m)
        for k, q in enumerate((None, q1, q2, q3)):
            peer = lax.rem(me + (TENSOR - k), TENSOR)
            at = pl.ds(pl.multiple_of(peer * own_rank, 8), own_rank)
            projected = crosses[i, at, :]
            if k == 0:
                m1, m2 = first[m], second[m]
            else:
                m1 = q[pl.ds(pl.multiple_of(m * own_rank, 8), own_rank), :]
                m2 = q[pl.ds(pl.multiple_of((mats + m) * own_rank, 8), own_rank), :]
            n1 = BETA_ONE * m1 + (1.0 - BETA_ONE) * projected
            n2 = BETA_TWO * m2 + (1.0 - BETA_TWO) * projected * projected
            if k == 0:
                new_first[m] = n1
                new_second[m] = n2
            directions[i, at, :] = n1 / c1 / (jnp.sqrt(n2 / c2) + EPSILON)
    for i, m in enumerate(which):
        update = dot3(split(state[i][2]), split(directions[i]))
        w = weight[m].astype(F32)
        weight_next[m] = (
            w - LEARN_RATE * (GALORE_SCALE * update + WEIGHT_DECAY * w)
        ).astype(BF16)


def shards(
    gradient,
    weight,
    projector,
    first_moment,
    squared_moment,
    step_count,
    norm_gains,
    gain_gradient,
    gain_first,
    gain_second,
):
    mats, rows, cols = gradient.shape
    rank = projector.shape[2]
    own_rank = first_moment.shape[1]
    half = rank // 2
    spread = lax.axis_size("shards")
    block = TENSOR * rows // spread
    shape = jax.ShapeDtypeStruct

    def shifted(x, k):
        return lax.ppermute(x, "tensor", [(i, (i + k) % TENSOR) for i in range(TENSOR)])

    def swapped(x, mask):
        return lax.ppermute(x, "tensor", [(i, i ^ mask) for i in range(TENSOR)])

    def call(kernel, out_shape, inputs, mib, in_specs=None, **more):
        outs = out_shape if isinstance(out_shape, tuple) else (out_shape,)
        got = pl.pallas_call(
            kernel,
            out_shape=outs,
            in_specs=in_specs or [VMEM] * len(inputs),
            out_specs=(VMEM,) * len(outs),
            compiler_params=pltpu.CompilerParams(vmem_limit_bytes=mib << 20),
            **more,
        )(*inputs)
        return got if isinstance(out_shape, tuple) else got[0]

    own, s1, s2, s3 = call(
        fold_kernel,
        (shape((cols, half), F32),) + (shape((rows + cols, half), F32),) * 3,
        (gradient, projector),
        8,
    )
    r2, r3, r1 = shifted(s2, 2), shifted(s3, 3), shifted(s1, 1)
    small = shape(norm_gains.shape, F32)
    pack, new_gains, new_gain_first, new_gain_second = call(
        pack_kernel,
        (shape((2 * mats * own_rank, cols), F32),) + (small,) * 3,
        (
            step_count, first_moment, squared_moment,
            norm_gains, gain_gradient, gain_first, gain_second,
        ),
        8,
        in_specs=[SMEM] + [VMEM] * 6,
    )
    q2, q3, q1 = shifted(pack, 2), shifted(pack, 3), shifted(pack, 1)

    ranged_part = call(
        range_kernel, shape((TENSOR * rows, half), F32), (gradient, own, r1, r2, r3), 8
    )
    parts = lax.all_to_all(ranged_part, "shards", 0, 0, tiled=True)
    blocks = call(
        spread_kernel, shape((spread, block, half), F32), (parts.reshape(spread, block, half),), 8
    )
    mine = lax.all_to_all(
        blocks.reshape(spread * block, half), "shards", 0, 0, tiled=True
    )
    gradients = (gradient, r1, r2, r3)
    message = shape((2 * half + rows, half), F32)
    beside = swapped(mine, 1)
    to_across, to_opposite = call(own_products_kernel, (message,) * 2, (mine,) + gradients, 8)
    across, opposite = swapped(to_across, 3), swapped(to_opposite, 2)
    joint, near = call(
        joint_products_kernel, (shape((half, half), F32), message), (mine, beside) + gradients, 8
    )
    joint_across = swapped(joint, 3)
    shapes = [weight, projector, first_moment, squared_moment]
    scratch = [
        pltpu.VMEM((rank, rank), F32),
        pltpu.VMEM((rank, cols), F32),
        pltpu.VMEM((rows, rank), F32),
    ]
    own_state = call(
        own_basis_kernel,
        (shape((rank, cols), F32), shape((rows, rank), F32)),
        (to_across, near, joint, mine),
        16,
        scratch_shapes=scratch,
    )
    weight_next, fresh_projector, new_first, new_second = call(
        finish_kernel,
        tuple(shape(x.shape, x.dtype) for x in shapes),
        tuple(own_state) + (
            opposite, across, joint_across,
            first_moment, squared_moment, weight, q1, q2, q3, step_count,
        ),
        24,
        in_specs=[VMEM] * 11 + [SMEM],
        scratch_shapes=[pltpu.VMEM((mats, rank, cols), F32)] * 2 + scratch,
    )
    return (
        weight_next,
        fresh_projector,
        new_first,
        new_second,
        new_gains,
        new_gain_first,
        new_gain_second,
    )


def solution(mesh):
    return jax.shard_map(
        shards,
        mesh=mesh,
        in_specs=(
            P("section", "tensor", "shards"),
            P("section", "tensor", "shards"),
            P("section", "tensor", None),
            P("section", "tensor", "shards"),
            P("section", "tensor", "shards"),
            P("section"),
            P("section", "tensor"),
            P("section", "tensor"),
            P("section", "tensor"),
            P("section", "tensor"),
        ),
        out_specs=(
            P("section", "tensor", "shards"),
            P("section", "tensor", None),
            P("section", "tensor", "shards"),
            P("section", "tensor", "shards"),
            P("section", "tensor"),
            P("section", "tensor"),
            P("section", "tensor"),
        ),
        check_vma=False,
    )
```
